32 devices in a mesh: pre: 4 (over x, core), dec: 8 (over z, y).
Axes of the slice: x: 2, y: 2, z: 4, core: 2. Of those that a mesh axis runs over, the one named last changes fastest.
Arguments:
- queries: bfloat16 [16, 128, 8192], P('pre', None, 'dec'), may hold values from -6 to 6, as said below
- branch_kv: bfloat16 [16, 128, 2048], P('pre', None, 'dec'), may hold values from -6 to 6
- pool_kv: bfloat16 [16, 128, 2048], P('pre', None, 'dec'), may hold values from -6 to 6, as said below
- page_lists: int32 [16, 16], replicated, may hold values from 0 to 15, as said below
- anc_len: int32 [16], replicated, may hold values from 1025 to 2048
- dec_owner: int32 [16], replicated, may hold values from 0 to 7, as said below
- output_projection_weight: bfloat16 [8192, 8192], P('dec'), may hold values from -0.0625 to 0.0625
Outputs:
- layer_out: bfloat16 [16, 128, 8192], P('pre', None, 'dec')
- decode_pages: bfloat16 [32, 128, 2048], P('dec', None, 'pre')
The draws below stay inside these ranges and needn't reach their ends.
Inputs may be any that keep to these rules, and one draw needn't show every extreme that they name: `queries`: floats within the range. `pool_kv`: floats within the range. `page_lists`: each branch lists distinct pages; the first half of the slots holds the same pages for every branch. `dec_owner`: the 4 branches of one prefill device (branches p * 4 on) go to distinct decode owners; one decode owner receives a branch from every prefill device.
All inputs are finite; a program needn't handle non-finite values.
Results may differ from the reference program's by a relative error of at most 0.024.
Values may be sent and summed in bfloat16 or wider, within the bound.
A program may use at most 128 MiB of HBM per device.

```python
import jax
import jax.numpy as jnp
from jax import lax

D = 8192
QH = 64
KVH = 8
HD = 128
PAGE = 128
NANC = 16
BR_DEV = 4
BRANCHES = 16
NPAGES = 16
N_PRE = 4
N_DEC = 8


def draw_queries(key, part):
    own_key = jax.random.fold_in(key, 11)
    shape = (BRANCHES, PAGE, QH, HD)
    base = jnp.clip(jax.random.normal(own_key, shape, jnp.float32), -6.0, 6.0)
    return base.reshape(BRANCHES, PAGE, QH * HD).astype(jnp.bfloat16)


def draw_pool_kv(key, part):
    own_key = jax.random.fold_in(key, 12)
    shape = (NPAGES, PAGE, KVH, 2, HD)
    base = jnp.clip(jax.random.normal(own_key, shape, jnp.float32), -6.0, 6.0)
    return base.reshape(NPAGES, PAGE, 2 * KVH * HD).astype(jnp.bfloat16)


def draw_page_lists(key, part):
    base_key = jax.random.fold_in(key, 13)
    order = jax.random.permutation(base_key, NPAGES).astype(jnp.int32)
    shared = NANC // 2
    root = order[:shared]
    rest = order[shared:]
    branch_keys = jax.random.split(jax.random.fold_in(base_key, 1), BRANCHES)
    tails = jax.vmap(lambda k: jax.random.permutation(k, rest)[:NANC - shared])(branch_keys)
    heads = jnp.broadcast_to(root[None, :], (BRANCHES, shared))
    return jnp.concatenate([heads, tails], 1).astype(jnp.int32)


def draw_dec_owner(key, part):
    base_key = jax.random.fold_in(key, 14)
    hot = jax.random.randint(base_key, (), 0, N_DEC).astype(jnp.int32)
    row_keys = jax.random.split(jax.random.fold_in(base_key, 1), N_PRE)

    def one_row(row_key):
        first, second = jax.random.split(row_key)
        others = jax.random.permutation(first, N_DEC - 1).astype(jnp.int32)
        others = others + (others >= hot).astype(jnp.int32)
        chosen = jnp.concatenate([hot[None], others[:BR_DEV - 1]])
        return jax.random.permutation(second, chosen)
    return jax.vmap(one_row)(row_keys).reshape(BRANCHES).astype(jnp.int32)


def place_ends(values, rng, least, high):
    longest = values.shape.index(max(values.shape))
    spots = []
    for shift in (0, 1):
        where = [jax.random.randint(jax.random.fold_in(rng, axis), (), 0, length) for axis, length in enumerate(values.shape)]
        where[longest] = (where[longest] + shift) % values.shape[longest]
        spots.append(tuple(where))
    return values.at[spots[0]].set(least).at[spots[1]].set(high)


def steps_of(key, shape, pieces, least, high):
    def one(dim, parts):
        steps = jax.random.uniform(jax.random.fold_in(jax.random.fold_in(key, 6), dim), (parts,), jnp.float32, least / len(pieces), high / len(pieces))
        return jnp.repeat(jnp.exp(steps), shape[dim] // parts).reshape((-1,) + (1,) * (len(shape) - dim - 1))

    gain = one(*pieces[0])
    for cut in pieces[1:]:
        gain = gain * one(*cut)
    return gain


def gaussian(key, extent, deviation, limit, cuts=(), held_as=jnp.bfloat16):
    values = jax.random.normal(key, extent, jnp.float32) * deviation
    if len(cuts) > 0:
        values = steps_of(key, extent, cuts, -0.22, 0.18) * values
    return jnp.clip(values, min=-limit, max=limit).astype(held_as)


def setup_inputs(seed: int = 0) -> dict:
    seeds = jax.random.split(jax.random.key(seed), 8)
    queries = draw_queries(jax.random.fold_in(seeds[7], 71), 0)
    branch_kv = gaussian(seeds[1], (BRANCHES, PAGE, 2 * KVH * HD), 1.0, 6.0, ((0, 4), (2, 8)))
    pool_kv = draw_pool_kv(jax.random.fold_in(seeds[7], 71), 0)
    page_lists = draw_page_lists(jax.random.fold_in(seeds[7], 71), 0)
    anc_len = place_ends(jax.random.randint(seeds[4], (BRANCHES,), NANC // 2 * PAGE + 1, NANC * PAGE + 1), jax.random.fold_in(seeds[4], 1), NANC // 2 * PAGE + 1, NANC * PAGE).astype(jnp.int32)
    dec_owner = draw_dec_owner(jax.random.fold_in(seeds[7], 71), 0)
    output_projection_weight = gaussian(seeds[6], (QH * HD, D), (QH * HD) ** -0.5, 0.0625, ((0, 8),))
    return dict(queries=queries, branch_kv=branch_kv, pool_kv=pool_kv, page_lists=page_lists, anc_len=anc_len, dec_owner=dec_owner, output_projection_weight=output_projection_weight)


def reference(queries, branch_kv, pool_kv, page_lists, anc_len, dec_owner, output_projection_weight):
    group = QH // KVH
    softmax_scale = HD ** -0.5

    def one_branch(item):
        q_rows, own_rows, pages, count = item
        query_vectors = q_rows.reshape(PAGE, QH, HD).astype(jnp.float32)
        ancestors = pool_kv[pages.astype(jnp.int32)].reshape(NANC * PAGE, KVH, 2, HD)
        own = own_rows.reshape(PAGE, KVH, 2, HD)
        keys = jnp.concatenate([ancestors[:, :, 0], own[:, :, 0]], 0)
        values = jnp.concatenate([ancestors[:, :, 1], own[:, :, 1]], 0)
        keys = jnp.repeat(keys, group, axis=1).astype(jnp.float32)
        values = jnp.repeat(values, group, axis=1).astype(jnp.float32)
        scores = jnp.einsum("qhd,khd->qhk", query_vectors, keys) * softmax_scale
        position = jnp.arange(NANC * PAGE, dtype=jnp.int32)
        earlier = jnp.broadcast_to((position < count)[None, :], (PAGE, NANC * PAGE))
        causal = jnp.arange(PAGE, dtype=jnp.int32)[None, :] <= jnp.arange(PAGE, dtype=jnp.int32)[:, None]
        allowed = jnp.concatenate([earlier, causal], 1)
        scores = jnp.where(allowed[:, None, :], scores, -jnp.inf)
        top = jnp.max(scores, axis=-1, keepdims=True)
        weights = jnp.exp(scores - top)
        running_denominator = jnp.sum(weights, axis=-1)
        probs = lax.optimization_barrier(weights.astype(jnp.bfloat16)).astype(jnp.float32)
        out = jnp.einsum("qhk,khd->qhd", probs, values) / running_denominator[..., None]
        return out.reshape(PAGE, QH * HD).astype(jnp.bfloat16)

    attention_result = lax.map(one_branch, (queries, branch_kv, page_lists, anc_len))
    attn_flat = attention_result.reshape(BRANCHES * PAGE, QH * HD)
    width = QH * HD // N_DEC

    def add_group(index, running_denominator):
        start = (index * width).astype(jnp.int32)
        cols = lax.dynamic_slice_in_dim(attn_flat, start, width, 1)
        rows = lax.dynamic_slice_in_dim(output_projection_weight, start, width, 0)
        exponent_term = jnp.dot(cols, rows, preferred_element_type=jnp.float32)
        exponent_term = lax.optimization_barrier(exponent_term.astype(jnp.bfloat16)).astype(jnp.float32)
        return running_denominator + exponent_term

    summed = lax.fori_loop(0, N_DEC, add_group, jnp.zeros((BRANCHES * PAGE, D), jnp.float32))
    layer_out = summed.astype(jnp.bfloat16).reshape(BRANCHES, PAGE, D)

    owners = dec_owner.reshape(N_PRE, BR_DEV)
    onehot = (owners[:, :, None] == jnp.arange(N_DEC, dtype=jnp.int32)[None, None, :]).astype(jnp.float32)
    kv_rows = branch_kv.reshape(N_PRE, BR_DEV, PAGE, 2 * KVH * HD).astype(jnp.float32)
    placed = jnp.einsum("pbo,pbqc->opqc", onehot, kv_rows)
    decode_pages = placed.reshape(N_DEC * N_PRE, PAGE, 2 * KVH * HD).astype(jnp.bfloat16)
    return layer_out, decode_pages
```

```python
import functools
import math

import jax
import jax.numpy as jnp
from jax import lax
from jax.experimental import pallas as pl
from jax.experimental.pallas import tpu as pltpu
from jax.sharding import PartitionSpec as P

HD = 128
MASKED = -1e30
SCALE = HD**-0.5 * math.log2(math.e)
FUSED = False
MESH = pl.DeviceIdType.MESH
VMEM = pl.BlockSpec(memory_space=pltpu.VMEM)


def from_partner(value, axis, stride):
    mask = 2**stride
    pairs = [(source, source ^ mask) for source in range(lax.axis_size(axis))]
    return lax.ppermute(value, axis, pairs)


def visibility_bias(lists, counts, page_count, page_len):
    slots = lists.shape[1]
    page_ids = jnp.arange(page_count, dtype=jnp.int32)
    reach = jnp.clip(
        counts[:, None] - jnp.arange(slots, dtype=jnp.int32)[None, :] * page_len, 0, page_len
    )
    match = lists[:, :, None] == page_ids[None, None, :]
    visible_count = jnp.sum(jnp.where(match, reach[:, :, None], 0), axis=1)
    tokens = jnp.arange(page_len, dtype=jnp.int32)
    allowed = tokens[None, None, :] < visible_count[:, :, None]
    allowed = allowed.reshape(lists.shape[0], 1, page_count * page_len)
    return jnp.where(allowed, 0.0, MASKED).astype(jnp.float32)


def exchange_kernel(
    n_pre, n_dec, pool_ref, bucket_ref, all_ref, pages_ref, own_sem, psend, precv, bsend, brecv
):
    pre = lax.axis_index("pre")
    dec = lax.axis_index("dec")
    count = pool_ref.shape[0]
    cols = bucket_ref.shape[2]
    ratio = n_dec // n_pre
    mine = pl.ds(pre * count, count)

    def pool_copy(k):
        return pltpu.make_async_remote_copy(
            src_ref=pool_ref,
            dst_ref=all_ref.at[mine],
            send_sem=psend.at[k],
            recv_sem=precv.at[k],
            device_id={"pre": lax.rem(pre + k, n_pre)},
            device_id_type=MESH,
        )

    for k in range(1, n_pre):
        pool_copy(k).start()
    own = pltpu.make_async_copy(pool_ref, all_ref.at[mine], own_sem)
    own.start()

    home = dec // ratio
    part = lax.rem(dec, ratio)
    column = pl.multiple_of(part * cols, 128)

    def bucket_copy(k):
        owner = lax.rem(dec + k, n_dec)
        return pltpu.make_async_remote_copy(
            src_ref=bucket_ref.at[owner],
            dst_ref=pages_ref.at[pre, :, pl.ds(column, cols)],
            send_sem=bsend.at[k],
            recv_sem=brecv.at[pre, part],
            device_id={"pre": home, "dec": owner},
            device_id_type=MESH,
        )

    for k in range(1, n_dec):
        bucket_copy(k).start()

    @pl.when(home == pre)
    def _():
        pltpu.make_async_copy(
            bucket_ref.at[dec], pages_ref.at[pre, :, pl.ds(column, cols)], brecv.at[pre, part]
        ).start()

    @pl.when(home != pre)
    def _():
        bucket_copy(0).start()

    own.wait()
    for k in range(1, n_pre):
        pool_copy(k).wait()
    for k in range(1, n_dec):
        bucket_copy(k).wait_send()

    @pl.when(home != pre)
    def _():
        bucket_copy(0).wait_send()

    for source in range(n_pre):
        for piece in range(ratio):
            place = pages_ref.at[source, :, pl.ds(piece * cols, cols)]
            pltpu.make_async_copy(place, place, brecv.at[source, piece]).wait()


def exchange(pool, buckets, n_pre, n_dec):
    count, page_len, width = pool.shape
    cols = buckets.shape[2]
    ratio = n_dec // n_pre
    return pl.pallas_call(
        functools.partial(exchange_kernel, n_pre, n_dec),
        out_shape=(
            jax.ShapeDtypeStruct((count * n_pre, page_len, width), pool.dtype),
            jax.ShapeDtypeStruct((n_pre, page_len, ratio * cols), buckets.dtype),
        ),
        in_specs=[VMEM] * 2,
        out_specs=(VMEM, VMEM),
        scratch_shapes=[
            pltpu.SemaphoreType.DMA,
            pltpu.SemaphoreType.DMA((n_pre,)),
            pltpu.SemaphoreType.DMA((n_pre,)),
            pltpu.SemaphoreType.DMA((n_dec,)),
            pltpu.SemaphoreType.DMA((n_pre, ratio)),
        ],
        compiler_params=pltpu.CompilerParams(has_side_effects=True),
        name="exchange",
    )(pool, buckets)


def load_values(pool_ref, values):
    pages, page_len, _ = pool_ref.shape
    values[:, :HD] = pool_ref[:, :, HD:].reshape(pages * page_len, HD)
    values[:, HD:] = jnp.ones((pages * page_len, HD), values.dtype)


def attend(branch, q_ref, own_ref, pool_ref, bias_ref, values, result_ref):
    pages, page_len, _ = pool_ref.shape
    heads = q_ref.shape[2] // HD
    pair = 2
    keys = pool_ref[:, :, :HD].reshape(pages * page_len, HD)
    own_keys = own_ref[branch, :, :HD]
    own_values = own_ref[branch, :, HD:]
    own_values = jnp.concatenate([own_values, jnp.ones_like(own_values)], 1)
    row = lax.broadcasted_iota(jnp.int32, (page_len, page_len), 0)
    col = lax.broadcasted_iota(jnp.int32, (page_len, page_len), 1)
    causal = jnp.where(col <= row, 0.0, MASKED)
    causal = jnp.concatenate([causal] * pair, 0)
    bias = bias_ref[branch]
    nt = (((1,), (1,)), ((), ()))

    def group(g, carry):
        start = pl.multiple_of(g * pair * HD, pair * HD)
        q = q_ref[branch, :, pl.ds(start, pair * HD)]
        q = jnp.concatenate([q[:, i * HD : (i + 1) * HD] for i in range(pair)], 0)
        far = lax.dot_general(q, keys, nt, preferred_element_type=jnp.float32) + bias
        near = lax.dot_general(q, own_keys, nt, preferred_element_type=jnp.float32) + causal
        top = jnp.maximum(
            jnp.max(far, axis=-1, keepdims=True), jnp.max(near, axis=-1, keepdims=True)
        )
        top = top * SCALE
        far = jnp.exp2(far * SCALE - top).astype(jnp.bfloat16)
        near = jnp.exp2(near * SCALE - top).astype(jnp.bfloat16)
        out = jnp.dot(far, values[...], preferred_element_type=jnp.float32)
        out = out + jnp.dot(near, own_values, preferred_element_type=jnp.float32)
        out = (out[:, :HD] / out[:, HD:]).astype(jnp.bfloat16)
        for i in range(pair):
            result_ref[branch, :, pl.ds(start + i * HD, HD)] = out[
                i * page_len : (i + 1) * page_len
            ]
        return carry

    lax.fori_loop(0, heads // pair, group, 0)


def attention_kernel(q_ref, own_ref, pool_ref, bias_ref, out_ref, values):
    load_values(pool_ref, values)

    def one(branch, carry):
        attend(branch, q_ref, own_ref, pool_ref, bias_ref, values, out_ref)
        return carry

    lax.fori_loop(0, q_ref.shape[0], one, 0)


def attention(queries, branch_kv, pool, bias):
    pages, page_len, _ = pool.shape
    return pl.pallas_call(
        attention_kernel,
        out_shape=jax.ShapeDtypeStruct(queries.shape, queries.dtype),
        in_specs=[VMEM] * 4,
        out_specs=VMEM,
        scratch_shapes=[pltpu.VMEM((pages * page_len, 2 * HD), jnp.bfloat16)],
        compiler_params=pltpu.CompilerParams(vmem_limit_bytes=48 * 2**20),
        name="attention",
    )(queries, branch_kv, pool, bias)


def project_kernel(n_dec, fused, *refs):
    if fused:
        q_ref, own_ref, pool_ref, bias_ref, w_ref, out_ref, values, attn, *refs = refs
    else:
        attn, w_ref, out_ref, *refs = refs
    wv, s1, r1, s2, r2, acc, wsem, s1sem, r1sem, s2sem, r2sem = refs
    branches = attn.shape[0]
    cols = out_ref.shape[2]
    half = n_dec // 2
    dec = lax.axis_index("dec")
    side = lax.rem(dec, 2)
    place = dec // 2
    partner = dec + 1 - 2 * side

    def target(t):
        return lax.rem(place + 1 + t, half)

    def load(slot, block):
        start = pl.multiple_of(block * cols, cols)
        return pltpu.make_async_copy(w_ref.at[:, pl.ds(start, cols)], wv.at[slot], wsem.at[slot])

    for t in range(half):
        load(t, 2 * target(t) + 1 - side).start()
    for t in range(half):
        load(half + t, 2 * target(t) + side).start()

    def first_copy(b, t):
        return pltpu.make_async_remote_copy(
            src_ref=s1.at[t, b],
            dst_ref=r1.at[t, b],
            send_sem=s1sem.at[t, b],
            recv_sem=r1sem.at[t, b],
            device_id={"dec": partner},
            device_id_type=MESH,
        )

    def second_copy(b, t):
        return pltpu.make_async_remote_copy(
            src_ref=s2.at[t, b],
            dst_ref=r2.at[t, b],
            send_sem=s2sem.at[t, b],
            recv_sem=r2sem.at[t, b],
            device_id={"dec": 2 * target(t) + side},
            device_id_type=MESH,
        )

    def loop(count, body):
        def step(i, carry):
            body(i)
            return carry

        lax.fori_loop(0, count, step, 0)

    def give(b):
        def one(t):
            s1[t, b] = jnp.dot(attn[b], wv[t], preferred_element_type=jnp.float32).astype(
                jnp.bfloat16
            )
            first_copy(b, t).start()

        loop(half, one)

    def take(b):
        def one(t):
            term = jnp.dot(attn[b], wv[half + t], preferred_element_type=jnp.float32)
            first_copy(b, t).wait_recv()
            s2[t, b] = (term + r1[t, b].astype(jnp.float32)).astype(jnp.bfloat16)
            second_copy(b, t).start()

        loop(half - 1, one)
        acc[b] = jnp.dot(attn[b], wv[n_dec - 1], preferred_element_type=jnp.float32)
        first_copy(b, half - 1).wait_recv()
        acc[b] += r1[half - 1, b].astype(jnp.float32)

    def finish(b):
        total = acc[b]
        for t in range(half - 1):
            second_copy(b, t).wait_recv()
            total = total + r2[t, b].astype(jnp.float32)
        out_ref[b] = total.astype(jnp.bfloat16)

    if fused:
        load_values(pool_ref, values)
        attend(0, q_ref, own_ref, pool_ref, bias_ref, values, attn)
    for slot in range(n_dec):
        load(slot, 0).wait()
    give(0)

    def middle(i):
        if fused:
            attend(i + 1, q_ref, own_ref, pool_ref, bias_ref, values, attn)
        give(i + 1)
        if fused:
            take(i)

    loop(branches - 1, middle)
    if fused:
        take(branches - 1)
    else:
        loop(branches, take)
    loop(branches, finish)

    def drain(b):
        for t in range(half):
            first_copy(b, t).wait_send()
        for t in range(half - 1):
            second_copy(b, t).wait_send()

    loop(branches, drain)


def project(inputs, weight, n_dec):
    fused = len(inputs) > 1
    branches, page_len, depth = inputs[0].shape
    cols = weight.shape[1] // n_dec
    half = n_dec // 2
    blocks = (half, branches, page_len, cols)
    head = []
    if fused:
        pages = inputs[2].shape[0]
        head = [
            pltpu.VMEM((pages * page_len, 2 * HD), jnp.bfloat16),
            pltpu.VMEM((branches, page_len, depth), jnp.bfloat16),
        ]
    return pl.pallas_call(
        functools.partial(project_kernel, n_dec, fused),
        out_shape=jax.ShapeDtypeStruct((branches, page_len, cols), jnp.bfloat16),
        in_specs=[VMEM] * len(inputs) + [pl.BlockSpec(memory_space=pl.ANY)],
        out_specs=VMEM,
        scratch_shapes=head
        + [
            pltpu.VMEM((n_dec, depth, cols), jnp.bfloat16),
            pltpu.VMEM(blocks, jnp.bfloat16),
            pltpu.VMEM(blocks, jnp.bfloat16),
            pltpu.VMEM((half - 1,) + blocks[1:], jnp.bfloat16),
            pltpu.VMEM((half - 1,) + blocks[1:], jnp.bfloat16),
            pltpu.VMEM(blocks[1:], jnp.float32),
            pltpu.SemaphoreType.DMA((n_dec,)),
            pltpu.SemaphoreType.DMA((half, branches)),
            pltpu.SemaphoreType.DMA((half, branches)),
            pltpu.SemaphoreType.DMA((half - 1, branches)),
            pltpu.SemaphoreType.DMA((half - 1, branches)),
        ],
        compiler_params=pltpu.CompilerParams(
            has_side_effects=True, vmem_limit_bytes=60 * 2**20
        ),
        name="project",
    )(*inputs, weight)


def on_device(
    queries, branch_kv, pool_kv, page_lists, anc_len, dec_owner, output_projection_weight
):
    n_pre = lax.axis_size("pre")
    n_dec = lax.axis_size("dec")
    pre_idx = lax.axis_index("pre")
    dec_idx = lax.axis_index("dec")
    branch_count, page_len, _ = queries.shape
    kv_cols = pool_kv.shape[2]
    if kv_cols < 2 * HD:
        other_pool, other_own = from_partner((pool_kv, branch_kv), "dec", 0)
        first_half = dec_idx % 2 == 0
        pool = jnp.where(
            first_half,
            jnp.concatenate([pool_kv, other_pool], 2),
            jnp.concatenate([other_pool, pool_kv], 2),
        )
        own = jnp.where(
            first_half,
            jnp.concatenate([branch_kv, other_own], 2),
            jnp.concatenate([other_own, branch_kv], 2),
        )
    else:
        pool, own = pool_kv, branch_kv

    start = pre_idx * branch_count
    my_lists = lax.dynamic_slice_in_dim(page_lists, start, branch_count, 0)
    my_counts = lax.dynamic_slice_in_dim(anc_len, start, branch_count, 0)
    owners = lax.dynamic_slice_in_dim(dec_owner, start, branch_count, 0)
    onehot = owners[:, None] == jnp.arange(n_dec, dtype=jnp.int32)[None, :]
    buckets = jnp.zeros((n_dec,) + branch_kv.shape[1:], branch_kv.dtype)
    for b in range(branch_count):
        buckets = jnp.where(onehot[b][:, None, None], branch_kv[b][None], buckets)

    pages, decode_pages = exchange(pool, buckets, n_pre, n_dec)
    bias = visibility_bias(my_lists, my_counts, pages.shape[0], page_len)
    if FUSED:
        inputs = (queries, own, pages, bias)
    else:
        inputs = (attention(queries, own, pages, bias),)
    layer_out = project(inputs, output_projection_weight, n_dec)
    return (layer_out, decode_pages)


def solution(mesh):
    in_specs = (
        P("pre", None, "dec"),
        P("pre", None, "dec"),
        P("pre", None, "dec"),
        P(),
        P(),
        P(),
        P("dec", None),
    )
    out_specs = (P("pre", None, "dec"), P("dec", None, "pre"))
    return jax.shard_map(
        on_device, mesh=mesh, in_specs=in_specs, out_specs=out_specs, check_vma=False
    )
```

```python
import functools
import math

import jax
import jax.numpy as jnp
from jax import lax
from jax.experimental import pallas as pl
from jax.experimental.pallas import tpu as pltpu
from jax.sharding import PartitionSpec as P

HD = 128
MASKED = -1e30
SCALE = HD**-0.5 * math.log2(math.e)
MESH = pl.DeviceIdType.MESH
VMEM = pl.BlockSpec(memory_space=pltpu.VMEM)


def from_partner(value, axis, stride):
    mask = 2**stride
    pairs = [(source, source ^ mask) for source in range(lax.axis_size(axis))]
    return lax.ppermute(value, axis, pairs)


def visibility_bias(lists, counts, page_count, page_len):
    slots = lists.shape[1]
    page_ids = jnp.arange(page_count, dtype=jnp.int32)
    reach = jnp.clip(
        counts[:, None] - jnp.arange(slots, dtype=jnp.int32)[None, :] * page_len, 0, page_len
    )
    match = lists[:, :, None] == page_ids[None, None, :]
    visible_count = jnp.sum(jnp.where(match, reach[:, :, None], 0), axis=1)
    tokens = jnp.arange(page_len, dtype=jnp.int32)
    allowed = tokens[None, None, :] < visible_count[:, :, None]
    allowed = allowed.reshape(lists.shape[0], 1, page_count * page_len)
    return jnp.where(allowed, 0.0, MASKED).astype(jnp.float32)


def load_values(pool_ref, values):
    pages, page_len, _ = pool_ref.shape
    values[:, :HD] = pool_ref[:, :, HD:].reshape(pages * page_len, HD)
    values[:, HD:] = jnp.ones((pages * page_len, HD), values.dtype)


def attend(branch, q_ref, own_ref, pool_ref, bias_ref, values, result_ref):
    pages, page_len, _ = pool_ref.shape
    heads = q_ref.shape[2] // HD
    pair = 2
    keys = pool_ref[:, :, :HD].reshape(pages * page_len, HD)
    own_keys = own_ref[branch, :, :HD]
    own_values = own_ref[branch, :, HD:]
    own_values = jnp.concatenate([own_values, jnp.ones_like(own_values)], 1)
    row = lax.broadcasted_iota(jnp.int32, (page_len, page_len), 0)
    col = lax.broadcasted_iota(jnp.int32, (page_len, page_len), 1)
    causal = jnp.where(col <= row, 0.0, MASKED)
    causal = jnp.concatenate([causal] * pair, 0)
    bias = bias_ref[branch]
    nt = (((1,), (1,)), ((), ()))

    def group(g, carry):
        start = pl.multiple_of(g * pair * HD, pair * HD)
        q = q_ref[branch, :, pl.ds(start, pair * HD)]
        q = jnp.concatenate([q[:, i * HD : (i + 1) * HD] for i in range(pair)], 0)
        far = lax.dot_general(q, keys, nt, preferred_element_type=jnp.float32) + bias
        near = lax.dot_general(q, own_keys, nt, preferred_element_type=jnp.float32) + causal
        top = jnp.maximum(
            jnp.max(far, axis=-1, keepdims=True), jnp.max(near, axis=-1, keepdims=True)
        )
        top = top * SCALE
        far = jnp.exp2(far * SCALE - top).astype(jnp.bfloat16)
        near = jnp.exp2(near * SCALE - top).astype(jnp.bfloat16)
        out = jnp.dot(far, values[...], preferred_element_type=jnp.float32)
        out = out + jnp.dot(near, own_values, preferred_element_type=jnp.float32)
        out = (out[:, :HD] / out[:, HD:]).astype(jnp.bfloat16)
        for i in range(pair):
            result_ref[branch, :, pl.ds(start + i * HD, HD)] = out[
                i * page_len : (i + 1) * page_len
            ]
        return carry

    lax.fori_loop(0, heads // pair, group, 0)


def bits_of(index, count):
    return [lax.rem(index // 2**k, 2) for k in range(count)]


def flipped(bits, rel):
    total = 0
    for k, bit in enumerate(bits):
        total = total + 2**k * (1 - bit if rel // 2**k % 2 else bit)
    return total


def halving(order):
    stages = []
    for s, bit in enumerate(order):
        done = [2**k for k in order[:s]]
        rest = [2**k for k in order[s + 1 :]]
        rels = [2**bit]
        for mask in reversed(rest):
            rels = [r + mask for r in rels] + rels
        stages.append([(r, bit, [r + m for m in done]) for r in rels])
    stages.append([(0, None, [2**k for k in order])])
    return stages


def layer_kernel(
    n_pre,
    n_dec,
    cuts,
    pool_ref,
    bucket_ref,
    q_hbm,
    own_hbm,
    bias_ref,
    w_ref,
    out_ref,
    pages_ref,
    all_ref,
    q_ref,
    own_ref,
    values,
    attn,
    wv,
    sent,
    got,
    load_sem,
    wsem,
    psend,
    precv,
    bsend,
    brecv,
    ssem,
    rsem,
):
    pre = lax.axis_index("pre")
    dec = lax.axis_index("dec")
    branches, page_len, cols = out_ref.shape
    count = pool_ref.shape[0]
    width = bucket_ref.shape[2]
    ratio = n_dec // n_pre
    chips = n_pre // 2
    chip = pre // 2
    core = lax.rem(pre, 2)
    log = n_dec.bit_length() - 1
    bits = bits_of(dec, log)

    def block_of(device):
        return pl.ds(device * count, count)

    def across(k):
        return pltpu.make_async_remote_copy(
            src_ref=pool_ref,
            dst_ref=all_ref.at[block_of(pre)],
            send_sem=psend.at[k],
            recv_sem=precv.at[k],
            device_id={"pre": lax.rem(chip + k, chips) * 2 + core},
            device_id_type=MESH,
        )

    def beside(k):
        where = all_ref.at[block_of(lax.rem(chip + chips - k, chips) * 2 + core)]
        return pltpu.make_async_remote_copy(
            src_ref=pool_ref if k == 0 else where,
            dst_ref=where,
            send_sem=psend.at[chips + k],
            recv_sem=precv.at[chips + k],
            device_id={"pre": chip * 2 + 1 - core},
            device_id_type=MESH,
        )

    for k in range(1, chips):
        across(k).start()
    beside(0).start()
    loads = [
        pltpu.make_async_copy(pool_ref, all_ref.at[block_of(pre)], load_sem.at[0]),
        pltpu.make_async_copy(q_hbm, q_ref, load_sem.at[1]),
        pltpu.make_async_copy(own_hbm, own_ref, load_sem.at[2]),
    ]
    for copy in loads:
        copy.start()

    def load(rel):
        start = pl.multiple_of(flipped(bits, rel) * cols, cols)
        return pltpu.make_async_copy(w_ref.at[:, pl.ds(start, cols)], wv.at[rel], wsem.at[rel])

    for rel in range(n_dec):
        load(rel).start()

    home = dec // ratio
    part = lax.rem(dec, ratio)
    column = pl.multiple_of(part * width, 128)

    def bucket_copy(k):
        owner = lax.rem(dec + k, n_dec)
        return pltpu.make_async_remote_copy(
            src_ref=bucket_ref.at[owner],
            dst_ref=pages_ref.at[pre, :, pl.ds(column, width)],
            send_sem=bsend.at[k],
            recv_sem=brecv.at[pre, part],
            device_id={"pre": home, "dec": owner},
            device_id_type=MESH,
        )

    for k in range(1, chips):
        across(k).wait_recv()
        beside(k).start()

    for k in range(1, n_dec):
        bucket_copy(k).start()

    @pl.when(home == pre)
    def _():
        pltpu.make_async_copy(
            bucket_ref.at[dec], pages_ref.at[pre, :, pl.ds(column, width)], brecv.at[pre, part]
        ).start()

    @pl.when(home != pre)
    def _():
        bucket_copy(0).start()

    for copy in loads:
        copy.wait()
    for k in range(chips):
        beside(k).wait_recv()
    load_values(all_ref, values)

    def piece(ref, rel, b, cut):
        return ref.at[rel, b, :, pl.ds(cuts[cut][0], cuts[cut][1])]

    def term_copy(rel, bit, b, cut):
        return pltpu.make_async_remote_copy(
            src_ref=piece(sent, rel, b, cut),
            dst_ref=piece(got, rel, b, cut),
            send_sem=ssem.at[cut, rel, b],
            recv_sem=rsem.at[cut, rel, b],
            device_id={"dec": flipped(bits, 2**bit)},
            device_id_type=MESH,
        )

    plans = [halving(order) for _, _, order in cuts]

    def senders(cut):
        return [(rel, bit) for stage in plans[cut][:-1] for rel, bit, _ in stage]

    bit_of = [dict(senders(cut)) for cut in range(len(cuts))]

    def run_stage(stage, b):
        for cut, (begin, size, _) in enumerate(cuts):
            for rel, bit, parts in plans[cut][stage]:
                for other in parts:
                    term_copy(other, bit_of[cut][other], b, cut).wait_recv()
                step = math.gcd(size, 256)

                def tile(i, carry, rel=rel, begin=begin, parts=parts, step=step, bit=bit):
                    at = pl.ds(pl.multiple_of(begin + i * step, step), step)
                    total = jnp.dot(
                        attn[b], wv[rel, :, at], preferred_element_type=jnp.float32
                    )
                    for other in parts:
                        total = total + got[other, b, :, at].astype(jnp.float32)
                    if bit is None:
                        out_ref[b, :, at] = total.astype(jnp.bfloat16)
                    else:
                        sent[rel, b, :, at] = total.astype(jnp.bfloat16)
                    return carry

                lax.fori_loop(0, size // step, tile, 0)
                if bit is not None:
                    term_copy(rel, bit, b, cut).start()

    def turn(i, carry):
        @pl.when(i < branches)
        def _():
            attend(i, q_ref, own_ref, all_ref, bias_ref, values, attn)

        @pl.when(i == 0)
        def _():
            for rel in range(n_dec):
                load(rel).wait()

        for stage in range(log + 1):
            @pl.when(jnp.logical_and(i >= stage, i < branches + stage))
            def _(stage=stage):
                run_stage(stage, i - stage)

        return carry

    lax.fori_loop(0, branches + log, turn, 0)

    def drain(b, carry):
        for cut in range(len(cuts)):
            for rel, bit in senders(cut):
                term_copy(rel, bit, b, cut).wait_send()
        return carry

    lax.fori_loop(0, branches, drain, 0)
    for k in range(1, chips):
        across(k).wait_send()
    for k in range(chips):
        beside(k).wait_send()
    for k in range(1, n_dec):
        bucket_copy(k).wait_send()

    @pl.when(home != pre)
    def _():
        bucket_copy(0).wait_send()

    for source in range(n_pre):
        for spot in range(ratio):
            where = pages_ref.at[source, :, pl.ds(spot * width, width)]
            pltpu.make_async_copy(where, where, brecv.at[source, spot]).wait()


def layer(pool, buckets, queries, own, bias, weight, n_pre, n_dec):
    branches, page_len, depth = queries.shape
    count = pool.shape[0]
    cols = weight.shape[1] // n_dec
    ratio = n_dec // n_pre
    log = n_dec.bit_length() - 1
    straight = tuple(range(log))
    other = (1, 0) + straight[2:]
    quarter = cols // 4
    cuts = ((0, quarter, other), (quarter, cols - quarter, straight))
    bf16 = jnp.bfloat16
    anywhere = pl.BlockSpec(memory_space=pl.ANY)
    return pl.pallas_call(
        functools.partial(layer_kernel, n_pre, n_dec, cuts),
        out_shape=(
            jax.ShapeDtypeStruct((branches, page_len, cols), bf16),
            jax.ShapeDtypeStruct((n_pre, page_len, ratio * buckets.shape[2]), bf16),
        ),
        in_specs=[anywhere] * 4 + [VMEM, anywhere],
        out_specs=(VMEM, VMEM),
        scratch_shapes=[
            pltpu.VMEM((count * n_pre,) + pool.shape[1:], bf16),
            pltpu.VMEM(queries.shape, bf16),
            pltpu.VMEM(own.shape, bf16),
            pltpu.VMEM((count * n_pre * page_len, 2 * HD), bf16),
            pltpu.VMEM(queries.shape, bf16),
            pltpu.VMEM((n_dec, depth, cols), bf16),
            pltpu.VMEM((n_dec, branches, page_len, cols), bf16),
            pltpu.VMEM((n_dec, branches, page_len, cols), bf16),
            pltpu.SemaphoreType.DMA((3,)),
            pltpu.SemaphoreType.DMA((n_dec,)),
            pltpu.SemaphoreType.DMA((n_pre,)),
            pltpu.SemaphoreType.DMA((n_pre,)),
            pltpu.SemaphoreType.DMA((n_dec,)),
            pltpu.SemaphoreType.DMA((n_pre, ratio)),
            pltpu.SemaphoreType.DMA((2, n_dec, branches)),
            pltpu.SemaphoreType.DMA((2, n_dec, branches)),
        ],
        compiler_params=pltpu.CompilerParams(
            has_side_effects=True, vmem_limit_bytes=62 * 2**20
        ),
        name="layer",
    )(pool, buckets, queries, own, bias, weight)


def on_device(
    queries, branch_kv, pool_kv, page_lists, anc_len, dec_owner, output_projection_weight
):
    n_pre = lax.axis_size("pre")
    n_dec = lax.axis_size("dec")
    pre_idx = lax.axis_index("pre")
    dec_idx = lax.axis_index("dec")
    branch_count, page_len, _ = queries.shape
    kv_cols = pool_kv.shape[2]
    if kv_cols < 2 * HD:
        other_pool, other_own = from_partner((pool_kv, branch_kv), "dec", 0)
        first_half = dec_idx % 2 == 0
        pool = jnp.where(
            first_half,
            jnp.concatenate([pool_kv, other_pool], 2),
            jnp.concatenate([other_pool, pool_kv], 2),
        )
        own = jnp.where(
            first_half,
            jnp.concatenate([branch_kv, other_own], 2),
            jnp.concatenate([other_own, branch_kv], 2),
        )
    else:
        pool, own = pool_kv, branch_kv

    start = pre_idx * branch_count
    my_lists = lax.dynamic_slice_in_dim(page_lists, start, branch_count, 0)
    my_counts = lax.dynamic_slice_in_dim(anc_len, start, branch_count, 0)
    owners = lax.dynamic_slice_in_dim(dec_owner, start, branch_count, 0)
    onehot = owners[:, None] == jnp.arange(n_dec, dtype=jnp.int32)[None, :]
    buckets = jnp.zeros((n_dec,) + branch_kv.shape[1:], branch_kv.dtype)
    for b in range(branch_count):
        buckets = jnp.where(onehot[b][:, None, None], branch_kv[b][None], buckets)

    bias = visibility_bias(my_lists, my_counts, pool.shape[0] * n_pre, page_len)
    layer_out, decode_pages = layer(
        pool, buckets, queries, own, bias, output_projection_weight, n_pre, n_dec
    )
    return (layer_out, decode_pages)


def solution(mesh):
    in_specs = (
        P("pre", None, "dec"),
        P("pre", None, "dec"),
        P("pre", None, "dec"),
        P(),
        P(),
        P(),
        P("dec", None),
    )
    out_specs = (P("pre", None, "dec"), P("dec", None, "pre"))
    return jax.shard_map(
        on_device, mesh=mesh, in_specs=in_specs, out_specs=out_specs, check_vma=False
    )
```

```python
import functools
import math

import jax
import jax.numpy as jnp
from jax import lax
from jax.experimental import pallas as pl
from jax.experimental.pallas import tpu as pltpu
from jax.sharding import PartitionSpec as P

HD = 128
MASKED = -1e30
SCALE = HD**-0.5 * math.log2(math.e)
MESH = pl.DeviceIdType.MESH
VMEM = pl.BlockSpec(memory_space=pltpu.VMEM)


def from_partner(value, axis, stride):
    mask = 2**stride
    pairs = [(source, source ^ mask) for source in range(lax.axis_size(axis))]
    return lax.ppermute(value, axis, pairs)


def visibility_bias(lists, counts, page_count, page_len):
    slots = lists.shape[1]
    page_ids = jnp.arange(page_count, dtype=jnp.int32)
    reach = jnp.clip(
        counts[:, None] - jnp.arange(slots, dtype=jnp.int32)[None, :] * page_len, 0, page_len
    )
    match = lists[:, :, None] == page_ids[None, None, :]
    visible_count = jnp.sum(jnp.where(match, reach[:, :, None], 0), axis=1)
    tokens = jnp.arange(page_len, dtype=jnp.int32)
    allowed = tokens[None, None, :] < visible_count[:, :, None]
    allowed = allowed.reshape(lists.shape[0], 1, page_count * page_len)
    return jnp.where(allowed, 0.0, MASKED).astype(jnp.float32)


def load_values(pool_ref, values):
    pages, page_len, _ = pool_ref.shape
    values[:, :HD] = pool_ref[:, :, HD:].reshape(pages * page_len, HD)
    values[:, HD:] = jnp.ones((pages * page_len, HD), values.dtype)


def attend(branch, q_ref, own_ref, pool_ref, bias_ref, values, result_ref):
    pages, page_len, _ = pool_ref.shape
    heads = q_ref.shape[2] // HD
    pair = 2
    keys = pool_ref[:, :, :HD].reshape(pages * page_len, HD)
    own_keys = own_ref[branch, :, :HD]
    own_values = own_ref[branch, :, HD:]
    own_values = jnp.concatenate([own_values, jnp.ones_like(own_values)], 1)
    row = lax.broadcasted_iota(jnp.int32, (page_len, page_len), 0)
    col = lax.broadcasted_iota(jnp.int32, (page_len, page_len), 1)
    causal = jnp.where(col <= row, 0.0, MASKED)
    causal = jnp.concatenate([causal] * pair, 0)
    bias = bias_ref[branch]
    nt = (((1,), (1,)), ((), ()))

    def group(g, carry):
        start = pl.multiple_of(g * pair * HD, pair * HD)
        q = q_ref[branch, :, pl.ds(start, pair * HD)]
        q = jnp.concatenate([q[:, i * HD : (i + 1) * HD] for i in range(pair)], 0)
        far = lax.dot_general(q, keys, nt, preferred_element_type=jnp.float32) + bias
        near = lax.dot_general(q, own_keys, nt, preferred_element_type=jnp.float32) + causal
        top = jnp.maximum(
            jnp.max(far, axis=-1, keepdims=True), jnp.max(near, axis=-1, keepdims=True)
        )
        top = top * SCALE
        far = jnp.exp2(far * SCALE - top).astype(jnp.bfloat16)
        near = jnp.exp2(near * SCALE - top).astype(jnp.bfloat16)
        out = jnp.dot(far, values[...], preferred_element_type=jnp.float32)
        out = out + jnp.dot(near, own_values, preferred_element_type=jnp.float32)
        out = (out[:, :HD] / out[:, HD:]).astype(jnp.bfloat16)
        for i in range(pair):
            result_ref[branch, :, pl.ds(start + i * HD, HD)] = out[
                i * page_len : (i + 1) * page_len
            ]
        return carry

    lax.fori_loop(0, heads // pair, group, 0)


def bits_of(index, count):
    return [lax.rem(index // 2**k, 2) for k in range(count)]


def flipped(bits, rel):
    total = 0
    for k, bit in enumerate(bits):
        total = total + 2**k * (1 - bit if rel // 2**k % 2 else bit)
    return total


def halving(order):
    stages = []
    for s, bit in enumerate(order):
        done = [2**k for k in order[:s]]
        rest = [2**k for k in order[s + 1 :]]
        rels = [2**bit]
        for mask in reversed(rest):
            rels = [r + mask for r in rels] + rels
        stages.append([(r, bit, [r + m for m in done]) for r in rels])
    stages.append([(0, None, [2**k for k in order])])
    return stages


def layer_kernel(
    n_pre,
    n_dec,
    cuts,
    pool_ref,
    bucket_ref,
    q_hbm,
    own_hbm,
    bias_ref,
    w_ref,
    out_ref,
    pages_ref,
    all_ref,
    q_ref,
    own_ref,
    values,
    attn,
    wv,
    sent,
    got,
    load_sem,
    wsem,
    psend,
    precv,
    bsend,
    brecv,
    ssem,
    rsem,
):
    pre = lax.axis_index("pre")
    dec = lax.axis_index("dec")
    branches, page_len, cols = out_ref.shape
    count = pool_ref.shape[0]
    width = bucket_ref.shape[2]
    ratio = n_dec // n_pre
    chips = n_pre // 2
    chip = pre // 2
    core = lax.rem(pre, 2)
    log = n_dec.bit_length() - 1
    bits = bits_of(dec, log)

    def block_of(device):
        return pl.ds(device * count, count)

    def across(k):
        return pltpu.make_async_remote_copy(
            src_ref=pool_ref,
            dst_ref=all_ref.at[block_of(pre)],
            send_sem=psend.at[k],
            recv_sem=precv.at[k],
            device_id={"pre": lax.rem(chip + k, chips) * 2 + core},
            device_id_type=MESH,
        )

    def beside(k):
        where = all_ref.at[block_of(lax.rem(chip + chips - k, chips) * 2 + core)]
        return pltpu.make_async_remote_copy(
            src_ref=pool_ref if k == 0 else where,
            dst_ref=where,
            send_sem=psend.at[chips + k],
            recv_sem=precv.at[chips + k],
            device_id={"pre": chip * 2 + 1 - core},
            device_id_type=MESH,
        )

    for k in range(1, chips):
        across(k).start()
    beside(0).start()
    loads = [
        pltpu.make_async_copy(pool_ref, all_ref.at[block_of(pre)], load_sem.at[0]),
        pltpu.make_async_copy(q_hbm, q_ref, load_sem.at[1]),
        pltpu.make_async_copy(own_hbm, own_ref, load_sem.at[2]),
    ]
    for copy in loads:
        copy.start()

    def load(rel):
        start = pl.multiple_of(flipped(bits, rel) * cols, cols)
        return pltpu.make_async_copy(w_ref.at[:, pl.ds(start, cols)], wv.at[rel], wsem.at[rel])

    for rel in range(n_dec):
        load(rel).start()

    home = dec // ratio
    part = lax.rem(dec, ratio)
    column = pl.multiple_of(part * width, 128)

    def bucket_copy(k):
        owner = lax.rem(dec + k, n_dec)
        return pltpu.make_async_remote_copy(
            src_ref=bucket_ref.at[owner],
            dst_ref=pages_ref.at[pre, :, pl.ds(column, width)],
            send_sem=bsend.at[k],
            recv_sem=brecv.at[pre, part],
            device_id={"pre": home, "dec": owner},
            device_id_type=MESH,
        )

    for k in range(1, chips):
        across(k).wait_recv()
        beside(k).start()

    for k in range(1, n_dec):
        bucket_copy(k).start()

    @pl.when(home == pre)
    def _():
        pltpu.make_async_copy(
            bucket_ref.at[dec], pages_ref.at[pre, :, pl.ds(column, width)], brecv.at[pre, part]
        ).start()

    @pl.when(home != pre)
    def _():
        bucket_copy(0).start()

    for copy in loads:
        copy.wait()
    for k in range(chips):
        beside(k).wait_recv()
    load_values(all_ref, values)

    def piece(ref, rel, b, cut):
        return ref.at[rel, b, :, pl.ds(cuts[cut][0], cuts[cut][1])]

    def term_copy(rel, bit, b, cut):
        return pltpu.make_async_remote_copy(
            src_ref=piece(sent, rel, b, cut),
            dst_ref=piece(got, rel, b, cut),
            send_sem=ssem.at[cut, rel, b],
            recv_sem=rsem.at[cut, rel, b],
            device_id={"dec": flipped(bits, 2**bit)},
            device_id_type=MESH,
        )

    plans = [halving(order) for _, _, order in cuts]

    def senders(cut):
        return [(rel, bit) for stage in plans[cut][:-1] for rel, bit, _ in stage]

    bit_of = [dict(senders(cut)) for cut in range(len(cuts))]

    def run_stage(stage, b):
        for cut, (begin, size, _) in enumerate(cuts):
            for rel, bit, parts in plans[cut][stage]:
                for other in parts:
                    term_copy(other, bit_of[cut][other], b, cut).wait_recv()
                step = math.gcd(size, 512)

                def tile(i, carry, rel=rel, begin=begin, parts=parts, step=step, bit=bit):
                    at = pl.ds(pl.multiple_of(begin + i * step, step), step)
                    total = jnp.dot(
                        attn[b], wv[rel, :, at], preferred_element_type=jnp.float32
                    )
                    for other in parts:
                        total = total + got[other, b, :, at].astype(jnp.float32)
                    if bit is None:
                        out_ref[b, :, at] = total.astype(jnp.bfloat16)
                    else:
                        sent[rel, b, :, at] = total.astype(jnp.bfloat16)
                    return carry

                lax.fori_loop(0, size // step, tile, 0)
                if bit is not None:
                    term_copy(rel, bit, b, cut).start()

    def turn(i, carry):
        @pl.when(i < branches)
        def _():
            attend(i, q_ref, own_ref, all_ref, bias_ref, values, attn)

        @pl.when(i == 0)
        def _():
            for rel in range(n_dec):
                load(rel).wait()

        for stage in range(log + 1):
            @pl.when(jnp.logical_and(i >= stage, i < branches + stage))
            def _(stage=stage):
                run_stage(stage, i - stage)

        return carry

    lax.fori_loop(0, branches + log, turn, 0)

    def drain(b, carry):
        for cut in range(len(cuts)):
            for rel, bit in senders(cut):
                term_copy(rel, bit, b, cut).wait_send()
        return carry

    lax.fori_loop(0, branches, drain, 0)
    for k in range(1, chips):
        across(k).wait_send()
    for k in range(chips):
        beside(k).wait_send()
    for k in range(1, n_dec):
        bucket_copy(k).wait_send()

    @pl.when(home != pre)
    def _():
        bucket_copy(0).wait_send()

    for source in range(n_pre):
        for spot in range(ratio):
            where = pages_ref.at[source, :, pl.ds(spot * width, width)]
            pltpu.make_async_copy(where, where, brecv.at[source, spot]).wait()


def layer(pool, buckets, queries, own, bias, weight, n_pre, n_dec):
    branches, page_len, depth = queries.shape
    count = pool.shape[0]
    cols = weight.shape[1] // n_dec
    ratio = n_dec // n_pre
    log = n_dec.bit_length() - 1
    straight = tuple(range(log))
    other = (1, 0) + straight[2:]
    part = cols // 2
    cuts = ((0, part, other), (part, cols - part, straight))
    bf16 = jnp.bfloat16
    anywhere = pl.BlockSpec(memory_space=pl.ANY)
    return pl.pallas_call(
        functools.partial(layer_kernel, n_pre, n_dec, cuts),
        out_shape=(
            jax.ShapeDtypeStruct((branches, page_len, cols), bf16),
            jax.ShapeDtypeStruct((n_pre, page_len, ratio * buckets.shape[2]), bf16),
        ),
        in_specs=[anywhere] * 4 + [VMEM, anywhere],
        out_specs=(VMEM, VMEM),
        scratch_shapes=[
            pltpu.VMEM((count * n_pre,) + pool.shape[1:], bf16),
            pltpu.VMEM(queries.shape, bf16),
            pltpu.VMEM(own.shape, bf16),
            pltpu.VMEM((count * n_pre * page_len, 2 * HD), bf16),
            pltpu.VMEM(queries.shape, bf16),
            pltpu.VMEM((n_dec, depth, cols), bf16),
            pltpu.VMEM((n_dec, branches, page_len, cols), bf16),
            pltpu.VMEM((n_dec, branches, page_len, cols), bf16),
            pltpu.SemaphoreType.DMA((3,)),
            pltpu.SemaphoreType.DMA((n_dec,)),
            pltpu.SemaphoreType.DMA((n_pre,)),
            pltpu.SemaphoreType.DMA((n_pre,)),
            pltpu.SemaphoreType.DMA((n_dec,)),
            pltpu.SemaphoreType.DMA((n_pre, ratio)),
            pltpu.SemaphoreType.DMA((2, n_dec, branches)),
            pltpu.SemaphoreType.DMA((2, n_dec, branches)),
        ],
        compiler_params=pltpu.CompilerParams(
            has_side_effects=True, vmem_limit_bytes=62 * 2**20
        ),
        name="layer",
    )(pool, buckets, queries, own, bias, weight)


def on_device(
    queries, branch_kv, pool_kv, page_lists, anc_len, dec_owner, output_projection_weight
):
    n_pre = lax.axis_size("pre")
    n_dec = lax.axis_size("dec")
    pre_idx = lax.axis_index("pre")
    dec_idx = lax.axis_index("dec")
    branch_count, page_len, _ = queries.shape
    kv_cols = pool_kv.shape[2]
    if kv_cols < 2 * HD:
        other_pool, other_own = from_partner((pool_kv, branch_kv), "dec", 0)
        first_half = dec_idx % 2 == 0
        pool = jnp.where(
            first_half,
            jnp.concatenate([pool_kv, other_pool], 2),
            jnp.concatenate([other_pool, pool_kv], 2),
        )
        own = jnp.where(
            first_half,
            jnp.concatenate([branch_kv, other_own], 2),
            jnp.concatenate([other_own, branch_kv], 2),
        )
    else:
        pool, own = pool_kv, branch_kv

    start = pre_idx * branch_count
    my_lists = lax.dynamic_slice_in_dim(page_lists, start, branch_count, 0)
    my_counts = lax.dynamic_slice_in_dim(anc_len, start, branch_count, 0)
    owners = lax.dynamic_slice_in_dim(dec_owner, start, branch_count, 0)
    onehot = owners[:, None] == jnp.arange(n_dec, dtype=jnp.int32)[None, :]
    buckets = jnp.zeros((n_dec,) + branch_kv.shape[1:], branch_kv.dtype)
    for b in range(branch_count):
        buckets = jnp.where(onehot[b][:, None, None], branch_kv[b][None], buckets)

    bias = visibility_bias(my_lists, my_counts, pool.shape[0] * n_pre, page_len)
    layer_out, decode_pages = layer(
        pool, buckets, queries, own, bias, output_projection_weight, n_pre, n_dec
    )
    return (layer_out, decode_pages)


def solution(mesh):
    in_specs = (
        P("pre", None, "dec"),
        P("pre", None, "dec"),
        P("pre", None, "dec"),
        P(),
        P(),
        P(),
        P("dec", None),
    )
    out_specs = (P("pre", None, "dec"), P("dec", None, "pre"))
    return jax.shard_map(
        on_device, mesh=mesh, in_specs=in_specs, out_specs=out_specs, check_vma=False
    )
```

```python
import functools
import math

import jax
import jax.numpy as jnp
from jax import lax
from jax.experimental import pallas as pl
from jax.experimental.pallas import tpu as pltpu
from jax.sharding import PartitionSpec as P

HD = 128
MASKED = -1e30
SCALE = HD**-0.5 * math.log2(math.e)
MESH = pl.DeviceIdType.MESH
VMEM = pl.BlockSpec(memory_space=pltpu.VMEM)


def from_partner(value, axis, stride):
    mask = 2**stride
    pairs = [(source, source ^ mask) for source in range(lax.axis_size(axis))]
    return lax.ppermute(value, axis, pairs)


def visibility_bias(lists, counts, page_count, page_len):
    slots = lists.shape[1]
    page_ids = jnp.arange(page_count, dtype=jnp.int32)
    reach = jnp.clip(
        counts[:, None] - jnp.arange(slots, dtype=jnp.int32)[None, :] * page_len, 0, page_len
    )
    match = lists[:, :, None] == page_ids[None, None, :]
    visible_count = jnp.sum(jnp.where(match, reach[:, :, None], 0), axis=1)
    tokens = jnp.arange(page_len, dtype=jnp.int32)
    allowed = tokens[None, None, :] < visible_count[:, :, None]
    allowed = allowed.reshape(lists.shape[0], 1, page_count * page_len)
    return jnp.where(allowed, 0.0, MASKED).astype(jnp.float32)


def load_values(pool_ref, values):
    pages, page_len, _ = pool_ref.shape
    values[:, :HD] = pool_ref[:, :, HD:].reshape(pages * page_len, HD)
    values[:, HD:] = jnp.ones((pages * page_len, HD), values.dtype)


def attend(branch, q_ref, own_ref, pool_ref, bias_ref, values, result_ref):
    pages, page_len, _ = pool_ref.shape
    heads = q_ref.shape[2] // HD
    pair = 2
    keys = pool_ref[:, :, :HD].reshape(pages * page_len, HD)
    own_keys = own_ref[branch, :, :HD]
    own_values = own_ref[branch, :, HD:]
    own_values = jnp.concatenate([own_values, jnp.ones_like(own_values)], 1)
    row = lax.broadcasted_iota(jnp.int32, (page_len, page_len), 0)
    col = lax.broadcasted_iota(jnp.int32, (page_len, page_len), 1)
    causal = jnp.where(col <= row, 0.0, MASKED)
    causal = jnp.concatenate([causal] * pair, 0)
    bias = bias_ref[branch]
    nt = (((1,), (1,)), ((), ()))

    def group(g, carry):
        start = pl.multiple_of(g * pair * HD, pair * HD)
        q = q_ref[branch, :, pl.ds(start, pair * HD)]
        q = jnp.concatenate([q[:, i * HD : (i + 1) * HD] for i in range(pair)], 0)
        far = lax.dot_general(q, keys, nt, preferred_element_type=jnp.float32) + bias
        near = lax.dot_general(q, own_keys, nt, preferred_element_type=jnp.float32) + causal
        top = jnp.maximum(
            jnp.max(far, axis=-1, keepdims=True), jnp.max(near, axis=-1, keepdims=True)
        )
        top = top * SCALE
        far = jnp.exp2(far * SCALE - top).astype(jnp.bfloat16)
        near = jnp.exp2(near * SCALE - top).astype(jnp.bfloat16)
        out = jnp.dot(far, values[...], preferred_element_type=jnp.float32)
        out = out + jnp.dot(near, own_values, preferred_element_type=jnp.float32)
        out = (out[:, :HD] / out[:, HD:]).astype(jnp.bfloat16)
        for i in range(pair):
            result_ref[branch, :, pl.ds(start + i * HD, HD)] = out[
                i * page_len : (i + 1) * page_len
            ]
        return carry

    lax.fori_loop(0, heads // pair, group, 0)


def bits_of(index, count):
    return [lax.rem(index // 2**k, 2) for k in range(count)]


def flipped(bits, rel):
    total = 0
    for k, bit in enumerate(bits):
        total = total + 2**k * (1 - bit if rel // 2**k % 2 else bit)
    return total


def halving(order):
    stages = []
    for s, bit in enumerate(order):
        done = [2**k for k in order[:s]]
        rest = [2**k for k in order[s + 1 :]]
        rels = [2**bit]
        for mask in reversed(rest):
            rels = [r + mask for r in rels] + rels
        stages.append([(r, bit, [r + m for m in done]) for r in rels])
    stages.append([(0, None, [2**k for k in order])])
    return stages


def layer_kernel(
    n_pre,
    n_dec,
    cuts,
    pool_ref,
    bucket_ref,
    q_hbm,
    own_hbm,
    bias_ref,
    w_ref,
    out_ref,
    pages_ref,
    all_ref,
    q_ref,
    own_ref,
    values,
    attn,
    wv,
    sent,
    got,
    load_sem,
    wsem,
    psend,
    precv,
    bsend,
    brecv,
    ssem,
    rsem,
):
    pre = lax.axis_index("pre")
    dec = lax.axis_index("dec")
    branches, page_len, cols = out_ref.shape
    count = pool_ref.shape[0]
    width = bucket_ref.shape[2]
    ratio = n_dec // n_pre
    chips = n_pre // 2
    chip = pre // 2
    core = lax.rem(pre, 2)
    log = n_dec.bit_length() - 1
    bits = bits_of(dec, log)

    def block_of(device):
        return pl.ds(device * count, count)

    def across(k):
        return pltpu.make_async_remote_copy(
            src_ref=pool_ref,
            dst_ref=all_ref.at[block_of(pre)],
            send_sem=psend.at[k],
            recv_sem=precv.at[k],
            device_id={"pre": lax.rem(chip + k, chips) * 2 + core},
            device_id_type=MESH,
        )

    def beside(k):
        where = all_ref.at[block_of(lax.rem(chip + chips - k, chips) * 2 + core)]
        return pltpu.make_async_remote_copy(
            src_ref=pool_ref if k == 0 else where,
            dst_ref=where,
            send_sem=psend.at[chips + k],
            recv_sem=precv.at[chips + k],
            device_id={"pre": chip * 2 + 1 - core},
            device_id_type=MESH,
        )

    for k in range(1, chips):
        across(k).start()
    beside(0).start()
    loads = [
        pltpu.make_async_copy(pool_ref, all_ref.at[block_of(pre)], load_sem.at[0]),
        pltpu.make_async_copy(q_hbm, q_ref, load_sem.at[1]),
        pltpu.make_async_copy(own_hbm, own_ref, load_sem.at[2]),
    ]
    for copy in loads:
        copy.start()

    def load(rel):
        start = pl.multiple_of(flipped(bits, rel) * cols, cols)
        return pltpu.make_async_copy(w_ref.at[:, pl.ds(start, cols)], wv.at[rel], wsem.at[rel])

    for rel in range(n_dec):
        load(rel).start()

    home = dec // ratio
    part = lax.rem(dec, ratio)
    column = pl.multiple_of(part * width, 128)

    def bucket_copy(k):
        owner = lax.rem(dec + k, n_dec)
        return pltpu.make_async_remote_copy(
            src_ref=bucket_ref.at[owner],
            dst_ref=pages_ref.at[pre, :, pl.ds(column, width)],
            send_sem=bsend.at[k],
            recv_sem=brecv.at[pre, part],
            device_id={"pre": home, "dec": owner},
            device_id_type=MESH,
        )

    for k in range(1, chips):
        across(k).wait_recv()
        beside(k).start()

    for k in range(1, n_dec):
        bucket_copy(k).start()

    @pl.when(home == pre)
    def _():
        pltpu.make_async_copy(
            bucket_ref.at[dec], pages_ref.at[pre, :, pl.ds(column, width)], brecv.at[pre, part]
        ).start()

    @pl.when(home != pre)
    def _():
        bucket_copy(0).start()

    for copy in loads:
        copy.wait()
    for k in range(chips):
        beside(k).wait_recv()
    load_values(all_ref, values)

    def piece(ref, rel, b, cut):
        return ref.at[rel, b, :, pl.ds(cuts[cut][0], cuts[cut][1])]

    def term_copy(rel, bit, b, cut):
        return pltpu.make_async_remote_copy(
            src_ref=piece(sent, rel, b, cut),
            dst_ref=piece(got, rel, b, cut),
            send_sem=ssem.at[cut, rel, b],
            recv_sem=rsem.at[cut, rel, b],
            device_id={"dec": flipped(bits, 2**bit)},
            device_id_type=MESH,
        )

    plans = [halving(order) for _, _, order in cuts]

    def senders(cut):
        return [(rel, bit) for stage in plans[cut][:-1] for rel, bit, _ in stage]

    bit_of = [dict(senders(cut)) for cut in range(len(cuts))]

    def run_stage(stage, b):
        for turns in zip(*[plan[stage] for plan in plans]):
            for cut, (rel, bit, parts) in enumerate(turns):
                begin, size, _ = cuts[cut]
                for other in parts:
                    term_copy(other, bit_of[cut][other], b, cut).wait_recv()
                step = math.gcd(size, 512)

                def tile(i, carry, rel=rel, begin=begin, parts=parts, step=step, bit=bit):
                    at = pl.ds(pl.multiple_of(begin + i * step, step), step)
                    total = jnp.dot(
                        attn[b], wv[rel, :, at], preferred_element_type=jnp.float32
                    )
                    for other in parts:
                        total = total + got[other, b, :, at].astype(jnp.float32)
                    if bit is None:
                        out_ref[b, :, at] = total.astype(jnp.bfloat16)
                    else:
                        sent[rel, b, :, at] = total.astype(jnp.bfloat16)
                    return carry

                lax.fori_loop(0, size // step, tile, 0)
                if bit is not None:
                    term_copy(rel, bit, b, cut).start()

    def turn(i, carry):
        @pl.when(i < branches)
        def _():
            attend(i, q_ref, own_ref, all_ref, bias_ref, values, attn)

        @pl.when(i == 0)
        def _():
            for rel in range(n_dec):
                load(rel).wait()

        for stage in range(log + 1):
            @pl.when(jnp.logical_and(i >= stage, i < branches + stage))
            def _(stage=stage):
                run_stage(stage, i - stage)

        return carry

    lax.fori_loop(0, branches + log, turn, 0)

    def drain(b, carry):
        for cut in range(len(cuts)):
            for rel, bit in senders(cut):
                term_copy(rel, bit, b, cut).wait_send()
        return carry

    lax.fori_loop(0, branches, drain, 0)
    for k in range(1, chips):
        across(k).wait_send()
    for k in range(chips):
        beside(k).wait_send()
    for k in range(1, n_dec):
        bucket_copy(k).wait_send()

    @pl.when(home != pre)
    def _():
        bucket_copy(0).wait_send()

    for source in range(n_pre):
        for spot in range(ratio):
            where = pages_ref.at[source, :, pl.ds(spot * width, width)]
            pltpu.make_async_copy(where, where, brecv.at[source, spot]).wait()


def layer(pool, buckets, queries, own, bias, weight, n_pre, n_dec):
    branches, page_len, depth = queries.shape
    count = pool.shape[0]
    cols = weight.shape[1] // n_dec
    ratio = n_dec // n_pre
    log = n_dec.bit_length() - 1
    straight = tuple(range(log))
    other = (1, 0) + straight[2:]
    part = cols // 2
    cuts = ((0, part, other), (part, cols - part, straight))
    bf16 = jnp.bfloat16
    anywhere = pl.BlockSpec(memory_space=pl.ANY)
    return pl.pallas_call(
        functools.partial(layer_kernel, n_pre, n_dec, cuts),
        out_shape=(
            jax.ShapeDtypeStruct((branches, page_len, cols), bf16),
            jax.ShapeDtypeStruct((n_pre, page_len, ratio * buckets.shape[2]), bf16),
        ),
        in_specs=[anywhere] * 4 + [VMEM, anywhere],
        out_specs=(VMEM, VMEM),
        scratch_shapes=[
            pltpu.VMEM((count * n_pre,) + pool.shape[1:], bf16),
            pltpu.VMEM(queries.shape, bf16),
            pltpu.VMEM(own.shape, bf16),
            pltpu.VMEM((count * n_pre * page_len, 2 * HD), bf16),
            pltpu.VMEM(queries.shape, bf16),
            pltpu.VMEM((n_dec, depth, cols), bf16),
            pltpu.VMEM((n_dec, branches, page_len, cols), bf16),
            pltpu.VMEM((n_dec, branches, page_len, cols), bf16),
            pltpu.SemaphoreType.DMA((3,)),
            pltpu.SemaphoreType.DMA((n_dec,)),
            pltpu.SemaphoreType.DMA((n_pre,)),
            pltpu.SemaphoreType.DMA((n_pre,)),
            pltpu.SemaphoreType.DMA((n_dec,)),
            pltpu.SemaphoreType.DMA((n_pre, ratio)),
            pltpu.SemaphoreType.DMA((2, n_dec, branches)),
            pltpu.SemaphoreType.DMA((2, n_dec, branches)),
        ],
        compiler_params=pltpu.CompilerParams(
            has_side_effects=True, vmem_limit_bytes=62 * 2**20
        ),
        name="layer",
    )(pool, buckets, queries, own, bias, weight)


def on_device(
    queries, branch_kv, pool_kv, page_lists, anc_len, dec_owner, output_projection_weight
):
    n_pre = lax.axis_size("pre")
    n_dec = lax.axis_size("dec")
    pre_idx = lax.axis_index("pre")
    dec_idx = lax.axis_index("dec")
    branch_count, page_len, _ = queries.shape
    kv_cols = pool_kv.shape[2]
    if kv_cols < 2 * HD:
        other_pool, other_own = from_partner((pool_kv, branch_kv), "dec", 0)
        first_half = dec_idx % 2 == 0
        pool = jnp.where(
            first_half,
            jnp.concatenate([pool_kv, other_pool], 2),
            jnp.concatenate([other_pool, pool_kv], 2),
        )
        own = jnp.where(
            first_half,
            jnp.concatenate([branch_kv, other_own], 2),
            jnp.concatenate([other_own, branch_kv], 2),
        )
    else:
        pool, own = pool_kv, branch_kv

    start = pre_idx * branch_count
    my_lists = lax.dynamic_slice_in_dim(page_lists, start, branch_count, 0)
    my_counts = lax.dynamic_slice_in_dim(anc_len, start, branch_count, 0)
    owners = lax.dynamic_slice_in_dim(dec_owner, start, branch_count, 0)
    onehot = owners[:, None] == jnp.arange(n_dec, dtype=jnp.int32)[None, :]
    buckets = jnp.zeros((n_dec,) + branch_kv.shape[1:], branch_kv.dtype)
    for b in range(branch_count):
        buckets = jnp.where(onehot[b][:, None, None], branch_kv[b][None], buckets)

    bias = visibility_bias(my_lists, my_counts, pool.shape[0] * n_pre, page_len)
    layer_out, decode_pages = layer(
        pool, buckets, queries, own, bias, output_projection_weight, n_pre, n_dec
    )
    return (layer_out, decode_pages)


def solution(mesh):
    in_specs = (
        P("pre", None, "dec"),
        P("pre", None, "dec"),
        P("pre", None, "dec"),
        P(),
        P(),
        P(),
        P("dec", None),
    )
    out_specs = (P("pre", None, "dec"), P("dec", None, "pre"))
    return jax.shard_map(
        on_device, mesh=mesh, in_specs=in_specs, out_specs=out_specs, check_vma=False
    )
```
